128 devices in a mesh: grp: 4 (over y), cp: 32 (over x, z, core).
Axes of the slice: x: 4, y: 4, z: 4, core: 2. Of those that a mesh axis runs over, the one named last changes fastest.
Arguments:
- queries: bfloat16 [4, 16384, 4096], P(None, ('grp', 'cp')), may hold values from -6 to 6, as said below
- keys: bfloat16 [4, 16384, 1024], P(None, ('grp', 'cp')), may hold values from -6 to 6, as said below
- values: bfloat16 [4, 16384, 1024], P(None, ('grp', 'cp')), may hold values from -6 to 6
- doc_lengths: int32 [4, 16], replicated, may hold values from 1 to 4096, 16384 in all within a row
Outputs:
- attended: bfloat16 [4, 16384, 4096], P(None, ('grp', 'cp'))
The draws below stay inside these ranges and needn't reach their ends.
Inputs may be any that keep to these rules, and one draw needn't show every extreme that they name: `doc_lengths`: each row holds the lengths of 16 documents that fill the stream's 16384 tokens exactly; the longest is exactly 4096 tokens. `queries`: entries of order one. `keys`: entries of order one.
All inputs are finite; a program needn't handle non-finite values.
Results may differ from the reference program's by a relative error of at most 0.0038.
Values may be sent and summed in bfloat16 or wider, within the bound.
No kernel may reach another device: no remote copies, remote signals or barrier semaphores. Data moves between devices by JAX's collectives and lax.ppermute only.
A program may use at most 128 MiB of HBM per device.

```python
import math
import jax
import jax.numpy as jnp
import numpy as np
from jax import lax

QUERY_HEADS = 32
KEY_VALUE_HEADS = 8
HEAD_WIDTH = 128
DOCS = 16
STREAM_COUNT = 4
STREAM_TOKENS = 16384
KVD = 1024
MOST = 4096


def draw_queries(key, part):
    array_extent = (STREAM_COUNT, STREAM_TOKENS, QUERY_HEADS * HEAD_WIDTH)
    result = jnp.clip(jax.random.normal(jax.random.fold_in(key, 1), array_extent, jnp.float32), -6.0, 6.0)
    return result.astype(jnp.bfloat16)


def draw_keys(key, part):
    array_extent = (STREAM_COUNT, STREAM_TOKENS, KEY_VALUE_HEADS * HEAD_WIDTH)
    result = jnp.clip(jax.random.normal(jax.random.fold_in(key, 2), array_extent, jnp.float32), -6.0, 6.0)
    return result.astype(jnp.bfloat16)


def shard_levels(stream_key, extent, shards, smallest, top_value):
    level = 1.0
    for axis_at, parts in shards:
        steps = jax.random.uniform(jax.random.fold_in(jax.random.fold_in(stream_key, 6), axis_at), (parts,), jnp.float32, smallest / len(shards), top_value / len(shards))
        level = level * jnp.repeat(jnp.exp(steps), extent[axis_at] // parts).reshape((-1,) + (1,) * (len(extent) - 1 - axis_at))
    return level


def length_profile(number_of, total, bound, slope):
    weights = [(1 << 20) // math.isqrt(standing ** slope) + 1 for standing in range(2, number_of + 1)]
    surplus, counts = total - bound - (number_of - 1), [1] * (number_of - 1)
    while surplus > 0:
        candidates = [i for i in range(number_of - 1) if counts[i] < bound]
        whole, remaining = sum([weights[i] for i in candidates]), surplus
        for i in candidates:
            more = min(bound - counts[i], max(1, remaining * weights[i] // whole), surplus)
            counts[i] = counts[i] + more
            surplus = surplus - more
    return np.array([bound] + counts)


def uneven_parts(rng, amount, total, bound, skew):
    if amount == 2:
        one = jax.random.randint(rng, (), max(1, total - bound), min(bound, total - 1) + 1)
        return jnp.stack([one, total - one])
    sizes = jnp.asarray(length_profile(amount, total, bound, skew), jnp.int32)
    twos = (amount - 1) // 2
    giver, receiver = sizes[1:1 + 2 * twos:2], sizes[2:2 + 2 * twos:2]
    slack = jnp.minimum(giver - 1, bound - receiver)
    passed = jax.random.randint(jax.random.fold_in(rng, 1), (twos,), 0, 1 << 20) % (slack + 1)
    sizes = sizes.at[1:1 + 2 * twos:2].set(giver - passed).at[2:2 + 2 * twos:2].set(receiver + passed)
    return sizes[jax.random.permutation(jax.random.fold_in(rng, 2), amount)]


def gaussian(own_key, dims, deviation, most, shards=(), held_as=jnp.bfloat16):
    entries = deviation * jax.random.normal(own_key, dims, jnp.float32)
    if shards:
        entries = entries * shard_levels(own_key, dims, shards, -0.22, 0.18)
    return jnp.clip(entries, -most, most).astype(held_as)


def setup_inputs(seed: int = 0) -> dict:
    key_list = jax.random.split(jax.random.key(seed), 5)
    return {
        "queries": draw_queries(jax.random.fold_in(key_list[4], 71), 0),
        "keys": draw_keys(jax.random.fold_in(key_list[4], 71), 0),
        "values": gaussian(key_list[2], (STREAM_COUNT, STREAM_TOKENS, KVD), 1.0, 6.0, ((1, 128),)),
        "doc_lengths": jax.vmap(lambda own: uneven_parts(own, DOCS, STREAM_TOKENS, MOST, 2))(jax.random.split(key_list[3], STREAM_COUNT)).reshape((STREAM_COUNT, DOCS)).astype(jnp.int32),
    }


def doc_index(lengths_row, positions):
    ends = jnp.cumsum(lengths_row)
    return jnp.sum((positions[:, None] >= ends[None, :]).astype(jnp.int32), axis=1)


def reference(queries, keys, values, doc_lengths):
    group_count = QUERY_HEADS // KEY_VALUE_HEADS
    scale = HEAD_WIDTH ** -0.5
    query_block_rows = min(256, STREAM_TOKENS)
    visible_span = min(MOST + query_block_rows, STREAM_TOKENS)

    def one_stream(bundle):
        query_rows, key_rows, value_rows, lengths_row = bundle
        positions = jnp.arange(STREAM_TOKENS, dtype=jnp.int32)
        docs = doc_index(lengths_row, positions)

        def one_block(begin):
            first = jnp.clip(begin + query_block_rows - visible_span, 0, STREAM_TOKENS - visible_span).astype(jnp.int32)
            key_portion = lax.dynamic_slice_in_dim(key_rows, first, visible_span, 0)
            value_portion = lax.dynamic_slice_in_dim(value_rows, first, visible_span, 0)
            heads_of_key = key_portion.reshape(visible_span, KEY_VALUE_HEADS, HEAD_WIDTH).astype(jnp.float32)
            heads_of_value = value_portion.reshape(visible_span, KEY_VALUE_HEADS, HEAD_WIDTH).astype(jnp.float32)
            key_pos = lax.dynamic_slice_in_dim(positions, first, visible_span, 0)
            key_doc = lax.dynamic_slice_in_dim(docs, first, visible_span, 0)
            block_of_queries = lax.dynamic_slice_in_dim(query_rows, begin, query_block_rows, 0)
            block_of_queries = block_of_queries.reshape(query_block_rows, KEY_VALUE_HEADS, group_count, HEAD_WIDTH).astype(jnp.float32)
            query_pos = begin + jnp.arange(query_block_rows, dtype=jnp.int32)
            query_doc = lax.dynamic_slice_in_dim(docs, begin, query_block_rows, 0)
            allowed = (key_pos[None, :] <= query_pos[:, None]) & (key_doc[None, :] == query_doc[:, None])
            scores = jnp.einsum("qhgd,khd->hgqk", block_of_queries, heads_of_key) * scale
            scores = jnp.where(allowed, scores, -1e30)
            largest = jnp.max(scores, axis=-1, keepdims=True)
            probs = jnp.where(allowed, jnp.exp(scores - largest), 0.0)
            total = jnp.sum(probs, axis=-1)
            weights = lax.optimization_barrier(probs.astype(jnp.bfloat16)).astype(jnp.float32)
            summed = jnp.einsum("hgqk,khd->hgqd", weights, heads_of_value)
            result = summed / total[..., None]
            return result.transpose(2, 0, 1, 3).reshape(query_block_rows, QUERY_HEADS * HEAD_WIDTH).astype(jnp.bfloat16)

        starts = jnp.arange(STREAM_TOKENS // query_block_rows, dtype=jnp.int32) * query_block_rows
        return lax.map(one_block, starts).reshape(STREAM_TOKENS, QUERY_HEADS * HEAD_WIDTH)

    return lax.map(one_stream, (queries, keys, values, doc_lengths))
```

```python
import functools

import jax
import jax.numpy as jnp
from jax import lax
from jax.experimental import pallas as pl
from jax.experimental.pallas import tpu as pltpu
from jax.sharding import PartitionSpec as P

QUERY_HEADS = 32
KEY_VALUE_HEADS = 8
WIDTH = 128
DOCS = 16
BLOCK = 128
RANKS = 32
CHUNK = RANKS * BLOCK
PAD = 256
TILE = 256
SPAN = 512
EDGE = 256
FACTOR = WIDTH ** (-0.5) * 1.4426950408889634
NEGATIVE = -1e30
LOW, HIGH = 1e-30, 1e30


def pack_keys(k_ref, v_ref, out_ref):
    for head in range(KEY_VALUE_HEADS):
        columns = slice(head * WIDTH, (head + 1) * WIDTH)
        out_ref[0, head, 0, 0] = k_ref[0, :, columns]
        out_ref[0, head, 0, 1] = v_ref[0, :, columns]


def pack_queries(q_ref, out_ref):
    for head in range(QUERY_HEADS):
        out_ref[0, head // 2, 0, head % 2] = q_ref[0, :, head * WIDTH : (head + 1) * WIDTH]


def unpack_outputs(in_ref, out_ref):
    for head in range(QUERY_HEADS):
        out_ref[0, :, head * WIDTH : (head + 1) * WIDTH] = in_ref[0, head // 2, 0, head % 2]


def attend(info, lengths, q_ref, mine, other, mine_before, other_before, o_ref, kbuf, vbuf, acc, start_of, top, ends, span_of):
    turn = pl.program_id(0)
    core, plane, pair = info[0], info[1], info[2]
    stream = pair * 2 + turn
    base = (plane - 1) * CHUNK

    def fill(before, now):
        kbuf[PAD : PAD + CHUNK] = before[:, :BLOCK].reshape(CHUNK, WIDTH)
        kbuf[PAD + CHUNK :] = now[:, :BLOCK].reshape(CHUNK, WIDTH)
        vbuf[PAD : PAD + CHUNK, :WIDTH] = before[:, BLOCK:].reshape(CHUNK, WIDTH)
        vbuf[PAD + CHUNK :, :WIDTH] = now[:, BLOCK:].reshape(CHUNK, WIDTH)

    @pl.when(turn == core)
    def _():
        fill(mine_before, mine)

    @pl.when(turn != core)
    def _():
        fill(other_before, other)

    @pl.when(turn == 0)
    def _():
        kbuf[:PAD] = jnp.zeros((PAD, WIDTH), jnp.bfloat16)
        vbuf[:PAD] = jnp.zeros((PAD, 2 * WIDTH), jnp.bfloat16)
        vbuf[PAD:, WIDTH:] = jnp.ones((2 * CHUNK, WIDTH), jnp.bfloat16)

    total = -base
    for doc in range(DOCS):
        total = total + lengths[stream, doc]
        ends[doc] = total

    def setup(tile):
        begin = CHUNK + tile * TILE
        first = -base
        last = -base
        for doc in range(DOCS):
            end = ends[doc]
            first = jnp.where(end <= begin, end, first)
            last = jnp.where(end <= begin + TILE - 1, end, last)
        rows = lax.broadcasted_iota(jnp.int32, (2, BLOCK, WIDTH), 0) * BLOCK + lax.broadcasted_iota(
            jnp.int32, (2, BLOCK, WIDTH), 1
        )

        @pl.when(first == last)
        def _():
            start_of[...] = jnp.full((2, BLOCK, WIDTH), first, jnp.int32)

        @pl.when(first != last)
        def _():
            start = jnp.full((2, BLOCK, WIDTH), first, jnp.int32)
            for doc in range(DOCS):
                end = ends[doc]
                start = jnp.where((end <= rows + begin) & (end > start), end, start)
            start_of[...] = start

        return begin, first, last

    def mask_of(begin, offset, width):
        shape = (2, 1, BLOCK, width)
        key = lax.broadcasted_iota(jnp.int32, shape, 3) + offset
        row = (
            lax.broadcasted_iota(jnp.int32, shape, 0) * BLOCK + lax.broadcasted_iota(jnp.int32, shape, 2)
        ) + begin
        start = jnp.concatenate([start_of[...]] * (width // WIDTH), axis=-1).reshape(shape)
        return (key >= start) & (key <= row)

    def scores_of(queries, offset, width):
        keys = kbuf[pl.ds(pl.multiple_of(offset + PAD, EDGE), width), :]
        return lax.dot_general(
            queries, keys, (((1,), (1,)), ((), ())), preferred_element_type=jnp.float32
        )

    def values_of(offset, width):
        return vbuf[pl.ds(pl.multiple_of(offset + PAD, EDGE), width), :]

    def fast(tile, carry):
        begin, first, last = setup(tile)
        queries = q_ref[pl.ds(tile * 2, 2)].reshape(4 * BLOCK, WIDTH)

        def edge(offset):
            scores = scores_of(queries, offset, EDGE) * FACTOR
            allowed = mask_of(begin, offset, EDGE)
            scores = jnp.where(allowed, scores.reshape(2, 2, BLOCK, EDGE), NEGATIVE)
            probs = jnp.exp2(scores.reshape(4 * BLOCK, EDGE)).astype(jnp.bfloat16)
            return jnp.dot(probs, values_of(offset, EDGE), preferred_element_type=jnp.float32)

        acc[...] = edge(begin)
        whole = jnp.maximum((begin - last) // SPAN, 0)

        def inner(step, carry):
            offset = begin - (step + 1) * SPAN
            probs = jnp.exp2(scores_of(queries, offset, SPAN) * FACTOR).astype(jnp.bfloat16)
            acc[...] += jnp.dot(probs, values_of(offset, SPAN), preferred_element_type=jnp.float32)
            return carry

        lax.fori_loop(0, whole, inner, 0)
        high = begin - whole * SPAN
        edges = (high - first + EDGE - 1) // EDGE

        def outer(step, carry):
            acc[...] += edge(high - (step + 1) * EDGE)
            return carry

        lax.fori_loop(0, edges, outer, 0)
        sums = acc[:, WIDTH:]
        o_ref[pl.ds(tile * 2, 2)] = (acc[:, :WIDTH] / sums).astype(jnp.bfloat16).reshape(2, 2, BLOCK, WIDTH)
        span_of[0] = jnp.minimum(span_of[0], jnp.min(sums.reshape(64, 8, WIDTH), axis=0))
        span_of[1] = jnp.maximum(span_of[1], jnp.max(sums.reshape(64, 8, WIDTH), axis=0))
        return carry

    def slow(tile, carry):
        begin, first, _ = setup(tile)
        queries = q_ref[pl.ds(tile * 2, 2)].reshape(4 * BLOCK, WIDTH)
        acc[...] = jnp.zeros_like(acc)
        top[...] = jnp.full_like(top, NEGATIVE)
        edges = (begin + TILE - first + EDGE - 1) // EDGE

        def absorb(step, carry):
            offset = begin + TILE - (step + 1) * EDGE
            scores = scores_of(queries, offset, EDGE) * FACTOR
            allowed = mask_of(begin, offset, EDGE)
            allowed = jnp.broadcast_to(allowed, (2, 2, BLOCK, EDGE)).reshape(4 * BLOCK, EDGE)
            scores = jnp.where(allowed, scores, NEGATIVE)
            before = top[...]
            peak = jnp.maximum(before, jnp.max(scores, axis=-1, keepdims=True))
            probs = jnp.where(allowed, jnp.exp2(scores - peak[:, :1]), 0.0).astype(jnp.bfloat16)
            shrink = jnp.exp2(before - peak)
            product = jnp.dot(probs, values_of(offset, EDGE), preferred_element_type=jnp.float32)
            acc[...] = acc[...] * shrink[:, :1] + product
            top[...] = peak
            return carry

        lax.fori_loop(0, edges, absorb, 0)
        o_ref[pl.ds(tile * 2, 2)] = (
            (acc[:, :WIDTH] / acc[:, WIDTH:]).astype(jnp.bfloat16).reshape(2, 2, BLOCK, WIDTH)
        )
        return carry

    span_of[0] = jnp.full((8, WIDTH), 1.0, jnp.float32)
    span_of[1] = jnp.full((8, WIDTH), 1.0, jnp.float32)
    lax.fori_loop(0, CHUNK // TILE, fast, 0)
    fits = (jnp.min(span_of[0]) >= LOW) & (jnp.max(span_of[1]) <= HIGH)

    @pl.when(jnp.logical_not(fits))
    def _():
        lax.fori_loop(0, CHUNK // TILE, slow, 0)


def estimate(flops, moved, powers=0):
    return pl.CostEstimate(flops=flops, bytes_accessed=moved, transcendentals=powers)


def on_device(queries, keys, values, doc_lengths):
    rank = lax.axis_index("cp")
    plane = lax.axis_index("grp")
    bf16 = jnp.bfloat16

    packed_kv = pl.pallas_call(
        pack_keys,
        grid=(4,),
        in_specs=[pl.BlockSpec((1, BLOCK, KEY_VALUE_HEADS * WIDTH), lambda s: (s, 0, 0))] * 2,
        out_specs=pl.BlockSpec((1, 8, 1, 2, BLOCK, WIDTH), lambda s: (s // 2, 0, s % 2, 0, 0, 0)),
        out_shape=jax.ShapeDtypeStruct((2, 8, 2, 2, BLOCK, WIDTH), bf16),
        cost_estimate=estimate(0, 4 << 20),
        name="pack_keys",
    )(keys, values)
    packed_q = pl.pallas_call(
        pack_queries,
        grid=(4,),
        in_specs=[pl.BlockSpec((1, BLOCK, QUERY_HEADS * WIDTH), lambda s: (s, 0, 0))],
        out_specs=pl.BlockSpec((1, 16, 1, 2, BLOCK, WIDTH), lambda s: (s // 2, 0, s % 2, 0, 0, 0)),
        out_shape=jax.ShapeDtypeStruct((2, 16, 2, 2, BLOCK, WIDTH), bf16),
        cost_estimate=estimate(0, 8 << 20),
        name="pack_queries",
    )(queries)

    swap = [(i, i ^ 1) for i in range(RANKS)]
    onward = [(i, (i + 1) % 4) for i in range(4)]
    mine = lax.all_to_all(packed_kv.reshape(RANKS, 2 * BLOCK, WIDTH), "cp", 0, 0, tiled=True)
    mine_before = lax.ppermute(mine, "grp", onward)
    other = lax.ppermute(mine, "cp", swap)
    other_before = lax.ppermute(mine_before, "cp", swap)
    got_q = lax.all_to_all(packed_q.reshape(RANKS, 4 * BLOCK, WIDTH), "cp", 0, 0, tiled=True)

    info = jnp.stack([rank % 2, plane, rank // 16]).astype(jnp.int32)
    whole = pl.BlockSpec((RANKS, 2 * BLOCK, WIDTH), lambda u, *_: (0, 0, 0), pipeline_mode=pl.Buffered(1))
    half = pl.BlockSpec((RANKS, None, 2, BLOCK, WIDTH), lambda u, *_: (0, u, 0, 0, 0))
    result = pl.pallas_call(
        attend,
        grid_spec=pltpu.PrefetchScalarGridSpec(
            num_scalar_prefetch=2,
            grid=(2,),
            in_specs=[half, whole, whole, whole, whole],
            out_specs=half,
            scratch_shapes=[
                pltpu.VMEM((PAD + 2 * CHUNK, WIDTH), bf16),
                pltpu.VMEM((PAD + 2 * CHUNK, 2 * WIDTH), bf16),
                pltpu.VMEM((4 * BLOCK, 2 * WIDTH), jnp.float32),
                pltpu.VMEM((2, BLOCK, WIDTH), jnp.int32),
                pltpu.VMEM((4 * BLOCK, WIDTH), jnp.float32),
                pltpu.SMEM((DOCS,), jnp.int32),
                pltpu.VMEM((2, 8, WIDTH), jnp.float32),
            ],
        ),
        out_shape=jax.ShapeDtypeStruct((RANKS, 2, 2, BLOCK, WIDTH), bf16),
        cost_estimate=estimate(20 << 30, 16 << 20, 20 << 20),
        compiler_params=pltpu.CompilerParams(vmem_limit_bytes=60 << 20),
        name="attend",
    )(info, doc_lengths, got_q.reshape(RANKS, 2, 2, BLOCK, WIDTH), mine, other, mine_before, other_before)

    back = lax.all_to_all(result.reshape(RANKS, 4 * BLOCK, WIDTH), "cp", 0, 0, tiled=True)
    return pl.pallas_call(
        unpack_outputs,
        grid=(4,),
        in_specs=[pl.BlockSpec((1, 16, 1, 2, BLOCK, WIDTH), lambda s: (s // 2, 0, s % 2, 0, 0, 0))],
        out_specs=pl.BlockSpec((1, BLOCK, QUERY_HEADS * WIDTH), lambda s: (s, 0, 0)),
        out_shape=jax.ShapeDtypeStruct((4, BLOCK, QUERY_HEADS * WIDTH), bf16),
        cost_estimate=estimate(0, 8 << 20),
        name="unpack_outputs",
    )(back.reshape(2, 16, 2, 2, BLOCK, WIDTH))


def solution(mesh):
    placed = P(None, ("grp", "cp"), None)
    return jax.shard_map(
        on_device,
        mesh=mesh,
        in_specs=(placed, placed, placed, P()),
        out_specs=placed,
        check_vma=False,
    )
```

```python
import functools

import jax
import jax.numpy as jnp
from jax import lax
from jax.experimental import pallas as pl
from jax.experimental.pallas import tpu as pltpu
from jax.sharding import PartitionSpec as P

QUERY_HEADS = 32
KEY_VALUE_HEADS = 8
WIDTH = 128
DOCS = 16
BLOCK = 128
RANKS = 32
CHUNK = RANKS * BLOCK
PAD = 256
TILE = 256
TILES = CHUNK // TILE
EDGE = 256
FACTOR = WIDTH ** (-0.5) * 1.4426950408889634
NEGATIVE = -1e30
LEAST = -(2**31)
LOW, HIGH = 1e-30, 1e30


def pack_keys(k_ref, v_ref, out_ref):
    for head in range(KEY_VALUE_HEADS):
        columns = slice(head * WIDTH, (head + 1) * WIDTH)
        out_ref[0, head, 0, 0] = k_ref[0, :, columns]
        out_ref[0, head, 0, 1] = v_ref[0, :, columns]


def pack_queries(q_ref, out_ref):
    for head in range(QUERY_HEADS):
        out_ref[0, head // 2, 0, head % 2] = q_ref[0, :, head * WIDTH : (head + 1) * WIDTH]


def unpack_outputs(in_ref, out_ref):
    for head in range(QUERY_HEADS):
        out_ref[0, :, head * WIDTH : (head + 1) * WIDTH] = in_ref[0, head // 2, 0, head % 2]


def attend(info, lengths, q_ref, mine, other, mine_before, other_before, o_ref, kbuf, vbuf, probs, acc, lows, reach, top, ends, low_of, docs_of, span_of):
    turn = pl.program_id(0)
    core, plane, pair = info[0], info[1], info[2]
    stream = pair * 2 + turn
    base = (plane - 1) * CHUNK

    def fill(before, now):
        kbuf[PAD : PAD + CHUNK] = before[:, :BLOCK].reshape(CHUNK, WIDTH)
        kbuf[PAD + CHUNK :] = now[:, :BLOCK].reshape(CHUNK, WIDTH)
        vbuf[PAD : PAD + CHUNK] = before[:, BLOCK:].reshape(CHUNK, WIDTH)
        vbuf[PAD + CHUNK :] = now[:, BLOCK:].reshape(CHUNK, WIDTH)

    @pl.when(turn == core)
    def _():
        fill(mine_before, mine)

    @pl.when(turn != core)
    def _():
        fill(other_before, other)

    rows = lax.broadcasted_iota(jnp.int32, (2, BLOCK, WIDTH), 0) * BLOCK + lax.broadcasted_iota(
        jnp.int32, (2, BLOCK, WIDTH), 1
    )
    lanes = lax.broadcasted_iota(jnp.int32, (2, BLOCK, WIDTH), 2)

    @pl.when(turn == 0)
    def _():
        kbuf[:PAD] = jnp.zeros((PAD, WIDTH), jnp.bfloat16)
        vbuf[:PAD] = jnp.zeros((PAD, WIDTH), jnp.bfloat16)

    acc[...] = jnp.zeros_like(acc)
    probs[...] = jnp.zeros_like(probs)

    total = -base
    for doc in range(DOCS):
        total = total + lengths[stream, doc]
        ends[doc] = total

    def survey(tile, blocks):
        begin = CHUNK + tile * TILE
        first, passed, within = -base, 0, 0
        for doc in range(DOCS):
            end = ends[doc]
            first = jnp.where(end <= begin, end, first)
            passed += (end <= begin).astype(jnp.int32)
            within += (end < begin + TILE).astype(jnp.int32)
        low = (first // EDGE) * EDGE
        low_of[tile] = low
        docs_of[0, tile] = first
        docs_of[1, tile] = passed
        docs_of[2, tile] = within
        return blocks + (begin - low) // EDGE + 1

    blocks = lax.fori_loop(0, TILES, survey, 0)

    def prepare(tile):
        begin = CHUNK + tile * TILE
        first = docs_of[0, tile]
        lows[...] = (first + LEAST) - lanes
        reach[...] = rows + (begin - first + LEAST)

        def mark(doc, carry):
            end = ends[doc]
            inside = rows + begin >= end
            lows[...] = jnp.where(inside, (end + LEAST) - lanes, lows[...])
            reach[...] = jnp.where(inside, rows + (begin - end + LEAST), reach[...])
            return carry

        lax.fori_loop(docs_of[1, tile], docs_of[2, tile], mark, 0)

    def scores_of(tile, offset):
        queries = q_ref[pl.ds(tile * 2, 2)].reshape(4 * BLOCK, WIDTH)
        keys = kbuf[pl.ds(pl.multiple_of(offset + PAD, EDGE), EDGE), :]
        return lax.dot_general(
            queries, keys, (((1,), (1,)), ((), ())), preferred_element_type=jnp.float32
        )

    def masked(scores, offset, piece, column):
        part = scores[piece * BLOCK : (piece + 1) * BLOCK, column * WIDTH : (column + 1) * WIDTH]
        allowed = (offset + column * WIDTH) - lows[piece // 2] <= reach[piece // 2]
        return jnp.where(allowed, part, NEGATIVE)

    def product_of(offset):
        values = vbuf[pl.ds(pl.multiple_of(offset + PAD, EDGE), EDGE), :]
        weights = jnp.concatenate([probs[0], probs[1]], axis=1)
        values = jnp.concatenate([values, jnp.ones((EDGE, WIDTH), jnp.bfloat16)], axis=1)
        return jnp.dot(weights, values, preferred_element_type=jnp.float32)

    def finish(tile):
        sums = acc[:, WIDTH:]
        o_ref[pl.ds(tile * 2, 2)] = (acc[:, :WIDTH] / sums).astype(jnp.bfloat16).reshape(2, 2, BLOCK, WIDTH)
        return sums

    def fast(step, carry):
        tile, offset, tile_before, offset_before, closes = carry
        acc[...] += product_of(offset_before)
        scores = scores_of(tile, offset)
        for piece in range(4):
            for column in range(2):
                part = jnp.exp2(masked(scores, offset, piece, column) * FACTOR)
                probs[column, piece * BLOCK : (piece + 1) * BLOCK] = part.astype(jnp.bfloat16)

        @pl.when(closes == 1)
        def _():
            sums = finish(tile_before)
            span_of[0] = jnp.minimum(span_of[0], jnp.min(sums.reshape(64, 8, WIDTH), axis=0))
            span_of[1] = jnp.maximum(span_of[1], jnp.max(sums.reshape(64, 8, WIDTH), axis=0))
            acc[...] = jnp.zeros_like(acc)

        ended = (offset <= low_of[tile]).astype(jnp.int32)
        tile_next = jnp.minimum(tile + ended, TILES - 1)
        offset_next = jnp.where(ended == 1, CHUNK + tile_next * TILE, offset - EDGE)

        @pl.when(ended == 1)
        def _():
            prepare(tile_next)

        return tile_next, offset_next, tile, offset, ended

    def slow(tile, carry):
        begin = CHUNK + tile * TILE
        prepare(tile)
        acc[...] = jnp.zeros_like(acc)
        top[...] = jnp.full_like(top, NEGATIVE)

        def absorb(step, carry):
            offset = begin - step * EDGE
            scores = scores_of(tile, offset)
            parts = [
                jnp.concatenate([masked(scores, offset, piece, column) * FACTOR for piece in range(4)], axis=0)
                for column in range(2)
            ]
            before = top[...]
            highest = jnp.max(jnp.maximum(parts[0], parts[1]), axis=-1, keepdims=True)
            peak = jnp.maximum(before, highest)
            for column in range(2):
                part = jnp.where(parts[column] > 0.5 * NEGATIVE * FACTOR, jnp.exp2(parts[column] - peak), 0.0)
                probs[column] = part.astype(jnp.bfloat16)
            shrink = jnp.exp2(before - peak)
            product = product_of(offset)
            for column in range(2):
                columns = slice(column * WIDTH, (column + 1) * WIDTH)
                acc[:, columns] = acc[:, columns] * shrink + product[:, columns]
            top[...] = peak
            return carry

        lax.fori_loop(0, (begin - low_of[tile]) // EDGE + 1, absorb, 0)
        finish(tile)
        return carry

    span_of[0] = jnp.full((8, WIDTH), 1.0, jnp.float32)
    span_of[1] = jnp.full((8, WIDTH), 1.0, jnp.float32)
    prepare(0)
    lax.fori_loop(0, blocks + 1, fast, (0, CHUNK, 0, CHUNK, 0))
    fits = (jnp.min(span_of[0]) >= LOW) & (jnp.max(span_of[1]) <= HIGH)

    @pl.when(jnp.logical_not(fits))
    def _():
        lax.fori_loop(0, TILES, slow, 0)


def estimate(flops, moved, powers=0):
    return pl.CostEstimate(flops=flops, bytes_accessed=moved, transcendentals=powers)


def on_device(queries, keys, values, doc_lengths):
    rank = lax.axis_index("cp")
    plane = lax.axis_index("grp")
    bf16 = jnp.bfloat16

    packed_kv = pl.pallas_call(
        pack_keys,
        grid=(4,),
        in_specs=[pl.BlockSpec((1, BLOCK, KEY_VALUE_HEADS * WIDTH), lambda s: (s, 0, 0))] * 2,
        out_specs=pl.BlockSpec((1, 8, 1, 2, BLOCK, WIDTH), lambda s: (s // 2, 0, s % 2, 0, 0, 0)),
        out_shape=jax.ShapeDtypeStruct((2, 8, 2, 2, BLOCK, WIDTH), bf16),
        cost_estimate=estimate(0, 4 << 20),
        name="pack_keys",
    )(keys, values)
    packed_q = pl.pallas_call(
        pack_queries,
        grid=(4,),
        in_specs=[pl.BlockSpec((1, BLOCK, QUERY_HEADS * WIDTH), lambda s: (s, 0, 0))],
        out_specs=pl.BlockSpec((1, 16, 1, 2, BLOCK, WIDTH), lambda s: (s // 2, 0, s % 2, 0, 0, 0)),
        out_shape=jax.ShapeDtypeStruct((2, 16, 2, 2, BLOCK, WIDTH), bf16),
        cost_estimate=estimate(0, 8 << 20),
        name="pack_queries",
    )(queries)

    swap = [(i, i ^ 1) for i in range(RANKS)]
    onward = [(i, (i + 1) % 4) for i in range(4)]
    mine = lax.all_to_all(packed_kv.reshape(RANKS, 2 * BLOCK, WIDTH), "cp", 0, 0, tiled=True)
    mine_before = lax.ppermute(mine, "grp", onward)
    other = lax.ppermute(mine, "cp", swap)
    other_before = lax.ppermute(mine_before, "cp", swap)
    got_q = lax.all_to_all(packed_q.reshape(RANKS, 4 * BLOCK, WIDTH), "cp", 0, 0, tiled=True)

    info = jnp.stack([rank % 2, plane, rank // 16]).astype(jnp.int32)
    whole = pl.BlockSpec((RANKS, 2 * BLOCK, WIDTH), lambda u, *_: (0, 0, 0), pipeline_mode=pl.Buffered(1))
    half = pl.BlockSpec((RANKS, None, 2, BLOCK, WIDTH), lambda u, *_: (0, u, 0, 0, 0))
    result = pl.pallas_call(
        attend,
        grid_spec=pltpu.PrefetchScalarGridSpec(
            num_scalar_prefetch=2,
            grid=(2,),
            in_specs=[half, whole, whole, whole, whole],
            out_specs=half,
            scratch_shapes=[
                pltpu.VMEM((PAD + 2 * CHUNK, WIDTH), bf16),
                pltpu.VMEM((PAD + 2 * CHUNK, WIDTH), bf16),
                pltpu.VMEM((2, 4 * BLOCK, WIDTH), bf16),
                pltpu.VMEM((4 * BLOCK, 2 * WIDTH), jnp.float32),
                pltpu.VMEM((2, BLOCK, WIDTH), jnp.int32),
                pltpu.VMEM((2, BLOCK, WIDTH), jnp.int32),
                pltpu.VMEM((4 * BLOCK, WIDTH), jnp.float32),
                pltpu.SMEM((DOCS,), jnp.int32),
                pltpu.SMEM((TILES,), jnp.int32),
                pltpu.SMEM((3, TILES), jnp.int32),
                pltpu.VMEM((2, 8, WIDTH), jnp.float32),
            ],
        ),
        out_shape=jax.ShapeDtypeStruct((RANKS, 2, 2, BLOCK, WIDTH), bf16),
        cost_estimate=estimate(20 << 30, 16 << 20, 20 << 20),
        compiler_params=pltpu.CompilerParams(vmem_limit_bytes=60 << 20),
        name="attend",
    )(info, doc_lengths, got_q.reshape(RANKS, 2, 2, BLOCK, WIDTH), mine, other, mine_before, other_before)

    back = lax.all_to_all(result.reshape(RANKS, 4 * BLOCK, WIDTH), "cp", 0, 0, tiled=True)
    return pl.pallas_call(
        unpack_outputs,
        grid=(4,),
        in_specs=[pl.BlockSpec((1, 16, 1, 2, BLOCK, WIDTH), lambda s: (s // 2, 0, s % 2, 0, 0, 0))],
        out_specs=pl.BlockSpec((1, BLOCK, QUERY_HEADS * WIDTH), lambda s: (s, 0, 0)),
        out_shape=jax.ShapeDtypeStruct((4, BLOCK, QUERY_HEADS * WIDTH), bf16),
        cost_estimate=estimate(0, 8 << 20),
        name="unpack_outputs",
    )(back.reshape(2, 16, 2, 2, BLOCK, WIDTH))


def solution(mesh):
    placed = P(None, ("grp", "cp"), None)
    return jax.shard_map(
        on_device,
        mesh=mesh,
        in_specs=(placed, placed, placed, P()),
        out_specs=placed,
        check_vma=False,
    )
```

```python
import functools

import jax
import jax.numpy as jnp
from jax import lax
from jax.experimental import pallas as pl
from jax.experimental.pallas import tpu as pltpu
from jax.sharding import PartitionSpec as P

QUERY_HEADS = 32
KEY_VALUE_HEADS = 8
WIDTH = 128
DOCS = 16
BLOCK = 128
RANKS = 32
CHUNK = RANKS * BLOCK
PAD = 512
TILE = 256
TILES = CHUNK // TILE
EDGE = 512
COLUMNS = EDGE // WIDTH
FACTOR = WIDTH ** (-0.5) * 1.4426950408889634
NEGATIVE = -1e30
LEAST = -(2**31)
LOW, HIGH = 1e-30, 1e30


def pack_keys(k_ref, v_ref, out_ref):
    for head in range(KEY_VALUE_HEADS):
        columns = slice(head * WIDTH, (head + 1) * WIDTH)
        out_ref[0, head, 0, 0] = k_ref[0, :, columns].T
        out_ref[0, head, 0, 1] = v_ref[0, :, columns]


def pack_queries(q_ref, out_ref):
    for head in range(QUERY_HEADS):
        out_ref[0, head // 2, 0, head % 2] = q_ref[0, :, head * WIDTH : (head + 1) * WIDTH]


def unpack_outputs(in_ref, out_ref):
    for head in range(QUERY_HEADS):
        out_ref[0, :, head * WIDTH : (head + 1) * WIDTH] = in_ref[0, head // 2, 0, head % 2]


def attend(info, lengths, q_ref, mine, other, mine_before, other_before, o_ref, kbuf, vbuf, probs, acc, sums, portion, lows, reach, top, ends, low_of, whole_of, docs_of, span_of):
    turn = pl.program_id(0)
    core, plane, pair = info[0], info[1], info[2]
    stream = pair * 2 + turn
    base = (plane - 1) * CHUNK

    def fill(before, now):
        kbuf[PAD // BLOCK : PAD // BLOCK + RANKS] = before[:, :BLOCK]
        kbuf[PAD // BLOCK + RANKS :] = now[:, :BLOCK]
        vbuf[PAD : PAD + CHUNK] = before[:, BLOCK:].reshape(CHUNK, WIDTH)
        vbuf[PAD + CHUNK :] = now[:, BLOCK:].reshape(CHUNK, WIDTH)

    @pl.when(turn == core)
    def _():
        fill(mine_before, mine)

    @pl.when(turn != core)
    def _():
        fill(other_before, other)

    rows = lax.broadcasted_iota(jnp.int32, (2, BLOCK, WIDTH), 0) * BLOCK + lax.broadcasted_iota(
        jnp.int32, (2, BLOCK, WIDTH), 1
    )
    lanes = lax.broadcasted_iota(jnp.int32, (2, BLOCK, WIDTH), 2)

    @pl.when(turn == 0)
    def _():
        kbuf[: PAD // BLOCK] = jnp.zeros((PAD // BLOCK, WIDTH, BLOCK), jnp.bfloat16)
        vbuf[:PAD] = jnp.zeros((PAD, WIDTH), jnp.bfloat16)

    acc[...] = jnp.zeros_like(acc)
    sums[...] = jnp.zeros_like(sums)
    probs[...] = jnp.zeros_like(probs)

    total = -base
    for doc in range(DOCS):
        total = total + lengths[stream, doc]
        ends[doc] = total

    def top_of(tile):
        return CHUNK + (tile + 1) * TILE - EDGE

    def survey(tile, blocks):
        begin = CHUNK + tile * TILE
        first, last, passed, within = -base, -base, 0, 0
        for doc in range(DOCS):
            end = ends[doc]
            first = jnp.where(end <= begin, end, first)
            last = jnp.where(end < begin + TILE, end, last)
            passed += (end <= begin).astype(jnp.int32)
            within += (end < begin + TILE).astype(jnp.int32)
        low = (first // TILE) * TILE
        low_of[tile] = low
        whole_of[tile] = last
        docs_of[0, tile] = first
        docs_of[1, tile] = passed
        docs_of[2, tile] = within
        return blocks + (begin + TILE - low + EDGE - 1) // EDGE

    blocks = lax.fori_loop(0, TILES, survey, 0)

    def prepare(tile):
        begin = CHUNK + tile * TILE
        first = docs_of[0, tile]
        lows[...] = (first + LEAST) - lanes
        reach[...] = rows + (begin - first + LEAST)

        def mark(doc, carry):
            end = ends[doc]
            inside = rows + begin >= end
            lows[...] = jnp.where(inside, (end + LEAST) - lanes, lows[...])
            reach[...] = jnp.where(inside, rows + (begin - end + LEAST), reach[...])
            return carry

        lax.fori_loop(docs_of[1, tile], docs_of[2, tile], mark, 0)

    def scores_of(tile, offset):
        at = (offset + PAD) // BLOCK
        queries = q_ref[pl.ds(tile * 2, 2)].reshape(4 * BLOCK, WIDTH)
        return [
            jnp.dot(
                queries,
                jnp.concatenate([kbuf[at + column], kbuf[at + column + 1]], axis=1),
                preferred_element_type=jnp.float32,
            )
            for column in range(0, COLUMNS, 2)
        ]

    def weigh(found, offset, uses_mask):
        for block in range(2):
            for row in range(0, BLOCK, 16):
                if uses_mask:
                    allowed = [
                        (offset + column * WIDTH) - lows[block, row : row + 16] <= reach[block, row : row + 16]
                        for column in range(COLUMNS)
                    ]
                for head in range(2):
                    rows_at = (block * 2 + head) * BLOCK + row
                    parts = []
                    for column in range(COLUMNS):
                        lane = column % 2 * WIDTH
                        part = found[column // 2][rows_at : rows_at + 16, lane : lane + WIDTH] * FACTOR
                        if uses_mask:
                            part = jnp.where(allowed[column], part, NEGATIVE)
                        part = jnp.exp2(part)
                        probs[column, rows_at : rows_at + 16] = part.astype(jnp.bfloat16)
                        parts.append(part)
                    sums[rows_at : rows_at + 16] += (parts[0] + parts[1]) + (parts[2] + parts[3])

    def product_of(offset):
        values = vbuf[pl.ds(pl.multiple_of(offset + PAD, TILE), EDGE), :]
        return [
            jnp.dot(
                jnp.concatenate([probs[column, half : half + 2 * BLOCK] for column in range(COLUMNS)], axis=1),
                values,
                preferred_element_type=jnp.float32,
            )
            for half in (0, 2 * BLOCK)
        ]

    def add(products):
        for half in range(2):
            acc[half * 2 * BLOCK : (half + 1) * 2 * BLOCK] += products[half]

    def close():
        total = jnp.sum(sums[...], axis=-1, keepdims=True)
        span_of[0] = jnp.minimum(span_of[0], jnp.min(total.reshape(64, 8, 1), axis=0))
        span_of[1] = jnp.maximum(span_of[1], jnp.max(total.reshape(64, 8, 1), axis=0))
        portion[...] = jnp.broadcast_to(1.0 / total, (4 * BLOCK, WIDTH))
        sums[...] = jnp.zeros_like(sums)

    def finish(tile):
        o_ref[pl.ds(tile * 2, 2)] = (acc[...] * portion[...]).astype(jnp.bfloat16).reshape(2, 2, BLOCK, WIDTH)
        acc[...] = jnp.zeros_like(acc)

    def fast(step, carry):
        tile, offset, tile_before, offset_before, closes = carry
        def both(uses_mask):
            found = scores_of(tile, offset)
            products = product_of(offset_before)
            weigh(found, offset, uses_mask)
            add(products)

        plain = (offset >= whole_of[tile]) & (offset < top_of(tile))

        @pl.when(plain)
        def _():
            both(False)

        @pl.when(jnp.logical_not(plain))
        def _():
            both(True)

        @pl.when(closes == 1)
        def _():
            finish(tile_before)

        ended = (offset <= low_of[tile]).astype(jnp.int32)
        tile_next = jnp.minimum(tile + ended, TILES - 1)
        offset_next = jnp.where(ended == 1, top_of(tile_next), offset - EDGE)

        @pl.when(ended == 1)
        def _():
            close()
            prepare(tile_next)

        return tile_next, offset_next, tile, offset, ended

    def slow(tile, carry):
        begin = CHUNK + tile * TILE
        prepare(tile)
        acc[...] = jnp.zeros_like(acc)
        sums[...] = jnp.zeros_like(sums)
        top[...] = jnp.full_like(top, NEGATIVE)

        def absorb(step, carry):
            offset = top_of(tile) - step * EDGE
            found = scores_of(tile, offset)
            for piece in range(4):
                at = slice(piece * BLOCK, (piece + 1) * BLOCK)
                parts = []
                for column in range(COLUMNS):
                    lane = column % 2 * WIDTH
                    part = found[column // 2][at, lane : lane + WIDTH]
                    allowed = (offset + column * WIDTH) - lows[piece // 2] <= reach[piece // 2]
                    parts.append(jnp.where(allowed, part * FACTOR, NEGATIVE))
                before = top[at]
                highest = jnp.maximum(jnp.maximum(parts[0], parts[1]), jnp.maximum(parts[2], parts[3]))
                peak = jnp.maximum(before, jnp.max(highest, axis=-1, keepdims=True))
                shrink = jnp.exp2(before - peak)
                total = jnp.zeros((BLOCK, WIDTH), jnp.float32)
                for column in range(COLUMNS):
                    part = jnp.where(parts[column] > 0.5 * NEGATIVE, jnp.exp2(parts[column] - peak), 0.0)
                    probs[column, at] = part.astype(jnp.bfloat16)
                    total = total + part
                sums[at] = sums[at] * shrink + total
                acc[at] = acc[at] * shrink
                top[at] = peak
            add(product_of(offset))
            return carry

        lax.fori_loop(0, (begin + TILE - low_of[tile] + EDGE - 1) // EDGE, absorb, 0)
        close()
        finish(tile)
        return carry

    span_of[0] = jnp.full((8, WIDTH), 1.0, jnp.float32)
    span_of[1] = jnp.full((8, WIDTH), 1.0, jnp.float32)
    prepare(0)
    lax.fori_loop(0, blocks + 1, fast, (0, top_of(0), 0, top_of(0), 0))
    fits = (jnp.min(span_of[0]) >= LOW) & (jnp.max(span_of[1]) <= HIGH)

    @pl.when(jnp.logical_not(fits))
    def _():
        lax.fori_loop(0, TILES, slow, 0)


def estimate(flops, moved, powers=0):
    return pl.CostEstimate(flops=flops, bytes_accessed=moved, transcendentals=powers)


def attention(info, doc_lengths, *arrays):
    whole = pl.BlockSpec((RANKS, 2 * BLOCK, WIDTH), lambda u, *_: (0, 0, 0), pipeline_mode=pl.Buffered(1))
    half = pl.BlockSpec((RANKS, None, 2, BLOCK, WIDTH), lambda u, *_: (0, u, 0, 0, 0))
    return pl.pallas_call(
        attend,
        grid_spec=pltpu.PrefetchScalarGridSpec(
            num_scalar_prefetch=2,
            grid=(2,),
            in_specs=[half, whole, whole, whole, whole],
            out_specs=half,
            scratch_shapes=[
                pltpu.VMEM(((PAD + 2 * CHUNK) // BLOCK, WIDTH, BLOCK), jnp.bfloat16),
                pltpu.VMEM((PAD + 2 * CHUNK, WIDTH), jnp.bfloat16),
                pltpu.VMEM((COLUMNS, 4 * BLOCK, WIDTH), jnp.bfloat16),
                pltpu.VMEM((4 * BLOCK, WIDTH), jnp.float32),
                pltpu.VMEM((4 * BLOCK, WIDTH), jnp.float32),
                pltpu.VMEM((4 * BLOCK, WIDTH), jnp.float32),
                pltpu.VMEM((2, BLOCK, WIDTH), jnp.int32),
                pltpu.VMEM((2, BLOCK, WIDTH), jnp.int32),
                pltpu.VMEM((4 * BLOCK, WIDTH), jnp.float32),
                pltpu.SMEM((DOCS,), jnp.int32),
                pltpu.SMEM((TILES,), jnp.int32),
                pltpu.SMEM((TILES,), jnp.int32),
                pltpu.SMEM((3, TILES), jnp.int32),
                pltpu.VMEM((2, 8, WIDTH), jnp.float32),
            ],
        ),
        out_shape=jax.ShapeDtypeStruct((RANKS, 2, 2, BLOCK, WIDTH), jnp.bfloat16),
        cost_estimate=estimate(20 << 30, 16 << 20, 20 << 20),
        compiler_params=pltpu.CompilerParams(vmem_limit_bytes=60 << 20),
        name="attend",
    )(info, doc_lengths, *arrays)


def on_device(queries, keys, values, doc_lengths):
    rank = lax.axis_index("cp")
    plane = lax.axis_index("grp")
    bf16 = jnp.bfloat16

    packed_kv = pl.pallas_call(
        pack_keys,
        grid=(4,),
        in_specs=[pl.BlockSpec((1, BLOCK, KEY_VALUE_HEADS * WIDTH), lambda s: (s, 0, 0))] * 2,
        out_specs=pl.BlockSpec((1, 8, 1, 2, BLOCK, WIDTH), lambda s: (s // 2, 0, s % 2, 0, 0, 0)),
        out_shape=jax.ShapeDtypeStruct((2, 8, 2, 2, BLOCK, WIDTH), bf16),
        cost_estimate=estimate(0, 4 << 20),
        name="pack_keys",
    )(keys, values)
    packed_q = pl.pallas_call(
        pack_queries,
        grid=(4,),
        in_specs=[pl.BlockSpec((1, BLOCK, QUERY_HEADS * WIDTH), lambda s: (s, 0, 0))],
        out_specs=pl.BlockSpec((1, 16, 1, 2, BLOCK, WIDTH), lambda s: (s // 2, 0, s % 2, 0, 0, 0)),
        out_shape=jax.ShapeDtypeStruct((2, 16, 2, 2, BLOCK, WIDTH), bf16),
        cost_estimate=estimate(0, 8 << 20),
        name="pack_queries",
    )(queries)

    swap = [(i, i ^ 1) for i in range(RANKS)]
    onward = [(i, (i + 1) % 4) for i in range(4)]
    mine = lax.all_to_all(packed_kv.reshape(RANKS, 2 * BLOCK, WIDTH), "cp", 0, 0, tiled=True)
    mine_before = lax.ppermute(mine, "grp", onward)
    other = lax.ppermute(mine, "cp", swap)
    other_before = lax.ppermute(mine_before, "cp", swap)
    got_q = lax.all_to_all(packed_q.reshape(RANKS, 4 * BLOCK, WIDTH), "cp", 0, 0, tiled=True)

    info = jnp.stack([rank % 2, plane, rank // 16]).astype(jnp.int32)
    result = attention(
        info, doc_lengths, got_q.reshape(RANKS, 2, 2, BLOCK, WIDTH), mine, other, mine_before, other_before
    )

    back = lax.all_to_all(result.reshape(RANKS, 4 * BLOCK, WIDTH), "cp", 0, 0, tiled=True)
    return pl.pallas_call(
        unpack_outputs,
        grid=(4,),
        in_specs=[pl.BlockSpec((1, 16, 1, 2, BLOCK, WIDTH), lambda s: (s // 2, 0, s % 2, 0, 0, 0))],
        out_specs=pl.BlockSpec((1, BLOCK, QUERY_HEADS * WIDTH), lambda s: (s, 0, 0)),
        out_shape=jax.ShapeDtypeStruct((4, BLOCK, QUERY_HEADS * WIDTH), bf16),
        cost_estimate=estimate(0, 8 << 20),
        name="unpack_outputs",
    )(back.reshape(2, 16, 2, 2, BLOCK, WIDTH))


def solution(mesh):
    placed = P(None, ("grp", "cp"), None)
    return jax.shard_map(
        on_device,
        mesh=mesh,
        in_specs=(placed, placed, placed, P()),
        out_specs=placed,
        check_vma=False,
    )
```

```python
import functools

import jax
import jax.numpy as jnp
from jax import lax
from jax.experimental import pallas as pl
from jax.experimental.pallas import tpu as pltpu
from jax.sharding import PartitionSpec as P

QUERY_HEADS = 32
KEY_VALUE_HEADS = 8
WIDTH = 128
DOCS = 16
BLOCK = 128
RANKS = 32
CHUNK = RANKS * BLOCK
PAD = 512
TILE = 256
TILES = CHUNK // TILE
EDGE = 512
COLUMNS = EDGE // WIDTH
FACTOR = WIDTH ** (-0.5) * 1.4426950408889634
NEGATIVE = -1e30
LEAST = -(2**31)
LOW, HIGH = 1e-30, 1e30


def pack_keys(k_ref, v_ref, out_ref):
    for head in range(KEY_VALUE_HEADS):
        columns = slice(head * WIDTH, (head + 1) * WIDTH)
        out_ref[0, head, 0, 0] = k_ref[0, :, columns].T
        out_ref[0, head, 0, 1] = v_ref[0, :, columns]


def pack_queries(q_ref, out_ref):
    for head in range(QUERY_HEADS):
        out_ref[0, head // 2, head % 2] = q_ref[0, :, head * WIDTH : (head + 1) * WIDTH]


def unpack_outputs(even_ref, odd_ref, out_ref):
    for turn, in_ref in enumerate((even_ref, odd_ref)):
        for head in range(QUERY_HEADS):
            out_ref[turn, :, head * WIDTH : (head + 1) * WIDTH] = in_ref[0, head // 2, head % 2]


def attend(info, lengths, q_ref, mine, other, mine_before, other_before, o_ref, kbuf, vbuf, probs, acc, sums, portion, lows, reach, top, ends, low_of, whole_of, docs_of, span_of, arrived):
    core, plane, pair, turn = info[0], info[1], info[2], info[3]
    stream = pair * 2 + turn
    base = (plane - 1) * CHUNK

    def fetch(before, now):
        copies = [
            pltpu.make_async_copy(source.at[:, pl.ds(half * BLOCK, BLOCK)], target.at[pl.ds(first, RANKS)], arrived.at[number])
            for number, (source, half, target, first) in enumerate(
                (
                    (before, 0, kbuf, PAD // BLOCK),
                    (now, 0, kbuf, PAD // BLOCK + RANKS),
                    (before, 1, vbuf, PAD // BLOCK),
                    (now, 1, vbuf, PAD // BLOCK + RANKS),
                )
            )
        ]
        for copy in copies:
            copy.start()
        for copy in copies:
            copy.wait()

    @pl.when(turn == core)
    def _():
        fetch(mine_before, mine)

    @pl.when(turn != core)
    def _():
        fetch(other_before, other)

    rows = lax.broadcasted_iota(jnp.int32, (2, BLOCK, WIDTH), 0) * BLOCK + lax.broadcasted_iota(
        jnp.int32, (2, BLOCK, WIDTH), 1
    )
    lanes = lax.broadcasted_iota(jnp.int32, (2, BLOCK, WIDTH), 2)

    kbuf[: PAD // BLOCK] = jnp.zeros((PAD // BLOCK, WIDTH, BLOCK), jnp.bfloat16)
    vbuf[: PAD // BLOCK] = jnp.zeros((PAD // BLOCK, BLOCK, WIDTH), jnp.bfloat16)
    acc[...] = jnp.zeros_like(acc)
    sums[...] = jnp.zeros_like(sums)
    probs[...] = jnp.zeros_like(probs)

    total = -base
    for doc in range(DOCS):
        total = total + lengths[stream, doc]
        ends[doc] = total

    def top_of(tile):
        return CHUNK + (tile + 1) * TILE - EDGE

    def survey(tile, blocks):
        begin = CHUNK + tile * TILE
        first, last, passed, within = -base, -base, 0, 0
        for doc in range(DOCS):
            end = ends[doc]
            first = jnp.where(end <= begin, end, first)
            last = jnp.where(end < begin + TILE, end, last)
            passed += (end <= begin).astype(jnp.int32)
            within += (end < begin + TILE).astype(jnp.int32)
        low = (first // TILE) * TILE
        low_of[tile] = low
        whole_of[tile] = last
        docs_of[0, tile] = first
        docs_of[1, tile] = passed
        docs_of[2, tile] = within
        return blocks + (begin + TILE - low + EDGE - 1) // EDGE

    blocks = lax.fori_loop(0, TILES, survey, 0)

    def prepare(tile):
        begin = CHUNK + tile * TILE
        first = docs_of[0, tile]
        lows[...] = (first + LEAST) - lanes
        reach[...] = rows + (begin - first + LEAST)

        def mark(doc, carry):
            end = ends[doc]
            inside = rows + begin >= end
            lows[...] = jnp.where(inside, (end + LEAST) - lanes, lows[...])
            reach[...] = jnp.where(inside, rows + (begin - end + LEAST), reach[...])
            return carry

        lax.fori_loop(docs_of[1, tile], docs_of[2, tile], mark, 0)

    def scores_of(tile, offset):
        at = (offset + PAD) // BLOCK
        queries = q_ref[pl.ds(tile * 2, 2)].reshape(4 * BLOCK, WIDTH)
        return [
            jnp.dot(
                queries,
                jnp.concatenate([kbuf[at + column], kbuf[at + column + 1]], axis=1),
                preferred_element_type=jnp.float32,
            )
            for column in range(0, COLUMNS, 2)
        ]

    def weigh(found, offset, uses_mask):
        for block in range(2):
            for row in range(0, BLOCK, 16):
                if uses_mask:
                    allowed = [
                        (offset + column * WIDTH) - lows[block, row : row + 16] <= reach[block, row : row + 16]
                        for column in range(COLUMNS)
                    ]
                for head in range(2):
                    rows_at = (block * 2 + head) * BLOCK + row
                    parts = []
                    for column in range(COLUMNS):
                        lane = column % 2 * WIDTH
                        part = found[column // 2][rows_at : rows_at + 16, lane : lane + WIDTH] * FACTOR
                        if uses_mask:
                            part = jnp.where(allowed[column], part, NEGATIVE)
                        part = jnp.exp2(part)
                        probs[column, rows_at : rows_at + 16] = part.astype(jnp.bfloat16)
                        parts.append(part)
                    sums[rows_at : rows_at + 16] += (parts[0] + parts[1]) + (parts[2] + parts[3])

    def product_of(offset):
        values = vbuf[pl.ds((offset + PAD) // BLOCK, EDGE // BLOCK)].reshape(EDGE, WIDTH)
        return [
            jnp.dot(
                jnp.concatenate([probs[column, half : half + 2 * BLOCK] for column in range(COLUMNS)], axis=1),
                values,
                preferred_element_type=jnp.float32,
            )
            for half in (0, 2 * BLOCK)
        ]

    def add(products):
        for half in range(2):
            acc[half * 2 * BLOCK : (half + 1) * 2 * BLOCK] += products[half]

    def close():
        total = jnp.sum(sums[...], axis=-1, keepdims=True)
        span_of[0] = jnp.minimum(span_of[0], jnp.min(total.reshape(64, 8, 1), axis=0))
        span_of[1] = jnp.maximum(span_of[1], jnp.max(total.reshape(64, 8, 1), axis=0))
        portion[...] = jnp.broadcast_to(1.0 / total, (4 * BLOCK, WIDTH))
        sums[...] = jnp.zeros_like(sums)

    def finish(tile):
        o_ref[pl.ds(tile * 2, 2)] = (acc[...] * portion[...]).astype(jnp.bfloat16).reshape(2, 2, BLOCK, WIDTH)
        acc[...] = jnp.zeros_like(acc)

    def fast(step, carry):
        tile, offset, tile_before, offset_before, closes = carry
        def both(uses_mask):
            found = scores_of(tile, offset)
            products = product_of(offset_before)
            weigh(found, offset, uses_mask)
            add(products)

        plain = (offset >= whole_of[tile]) & (offset < top_of(tile))

        @pl.when(plain)
        def _():
            both(False)

        @pl.when(jnp.logical_not(plain))
        def _():
            both(True)

        @pl.when(closes == 1)
        def _():
            finish(tile_before)

        ended = (offset <= low_of[tile]).astype(jnp.int32)
        tile_next = jnp.minimum(tile + ended, TILES - 1)
        offset_next = jnp.where(ended == 1, top_of(tile_next), offset - EDGE)

        @pl.when(ended == 1)
        def _():
            close()
            prepare(tile_next)

        return tile_next, offset_next, tile, offset, ended

    def slow(tile, carry):
        begin = CHUNK + tile * TILE
        prepare(tile)
        acc[...] = jnp.zeros_like(acc)
        sums[...] = jnp.zeros_like(sums)
        top[...] = jnp.full_like(top, NEGATIVE)

        def absorb(step, carry):
            offset = top_of(tile) - step * EDGE
            found = scores_of(tile, offset)
            for piece in range(4):
                at = slice(piece * BLOCK, (piece + 1) * BLOCK)
                parts = []
                for column in range(COLUMNS):
                    lane = column % 2 * WIDTH
                    part = found[column // 2][at, lane : lane + WIDTH]
                    allowed = (offset + column * WIDTH) - lows[piece // 2] <= reach[piece // 2]
                    parts.append(jnp.where(allowed, part * FACTOR, NEGATIVE))
                before = top[at]
                highest = jnp.maximum(jnp.maximum(parts[0], parts[1]), jnp.maximum(parts[2], parts[3]))
                peak = jnp.maximum(before, jnp.max(highest, axis=-1, keepdims=True))
                shrink = jnp.exp2(before - peak)
                total = jnp.zeros((BLOCK, WIDTH), jnp.float32)
                for column in range(COLUMNS):
                    part = jnp.where(parts[column] > 0.5 * NEGATIVE, jnp.exp2(parts[column] - peak), 0.0)
                    probs[column, at] = part.astype(jnp.bfloat16)
                    total = total + part
                sums[at] = sums[at] * shrink + total
                acc[at] = acc[at] * shrink
                top[at] = peak
            add(product_of(offset))
            return carry

        lax.fori_loop(0, (begin + TILE - low_of[tile] + EDGE - 1) // EDGE, absorb, 0)
        close()
        finish(tile)
        return carry

    span_of[0] = jnp.full((8, WIDTH), 1.0, jnp.float32)
    span_of[1] = jnp.full((8, WIDTH), 1.0, jnp.float32)
    prepare(0)
    lax.fori_loop(0, blocks + 1, fast, (0, top_of(0), 0, top_of(0), 0))
    fits = (jnp.min(span_of[0]) >= LOW) & (jnp.max(span_of[1]) <= HIGH)

    @pl.when(jnp.logical_not(fits))
    def _():
        lax.fori_loop(0, TILES, slow, 0)


def estimate(flops, moved, powers=0):
    return pl.CostEstimate(flops=flops, bytes_accessed=moved, transcendentals=powers)


def attention(info, doc_lengths, *arrays):
    anywhere = pl.BlockSpec(memory_space=pl.ANY)
    half = pl.BlockSpec((RANKS, 2, BLOCK, WIDTH), lambda u, *_: (0, 0, 0, 0), pipeline_mode=pl.Buffered(1))
    return pl.pallas_call(
        attend,
        grid_spec=pltpu.PrefetchScalarGridSpec(
            num_scalar_prefetch=2,
            grid=(1,),
            in_specs=[half, anywhere, anywhere, anywhere, anywhere],
            out_specs=half,
            scratch_shapes=[
                pltpu.VMEM(((PAD + 2 * CHUNK) // BLOCK, WIDTH, BLOCK), jnp.bfloat16),
                pltpu.VMEM(((PAD + 2 * CHUNK) // BLOCK, BLOCK, WIDTH), jnp.bfloat16),
                pltpu.VMEM((COLUMNS, 4 * BLOCK, WIDTH), jnp.bfloat16),
                pltpu.VMEM((4 * BLOCK, WIDTH), jnp.float32),
                pltpu.VMEM((4 * BLOCK, WIDTH), jnp.float32),
                pltpu.VMEM((4 * BLOCK, WIDTH), jnp.float32),
                pltpu.VMEM((2, BLOCK, WIDTH), jnp.int32),
                pltpu.VMEM((2, BLOCK, WIDTH), jnp.int32),
                pltpu.VMEM((4 * BLOCK, WIDTH), jnp.float32),
                pltpu.SMEM((DOCS,), jnp.int32),
                pltpu.SMEM((TILES,), jnp.int32),
                pltpu.SMEM((TILES,), jnp.int32),
                pltpu.SMEM((3, TILES), jnp.int32),
                pltpu.VMEM((2, 8, WIDTH), jnp.float32),
                pltpu.SemaphoreType.DMA((4,)),
            ],
        ),
        out_shape=jax.ShapeDtypeStruct((RANKS, 2, BLOCK, WIDTH), jnp.bfloat16),
        cost_estimate=estimate(20 << 30, 8 << 20, 10 << 20),
        compiler_params=pltpu.CompilerParams(vmem_limit_bytes=60 << 20),
        name="attend",
    )(info, doc_lengths, *arrays)


def on_device(queries, keys, values, doc_lengths):
    rank = lax.axis_index("cp")
    plane = lax.axis_index("grp")
    bf16 = jnp.bfloat16

    packed_kv = pl.pallas_call(
        pack_keys,
        grid=(4,),
        in_specs=[pl.BlockSpec((1, BLOCK, KEY_VALUE_HEADS * WIDTH), lambda s: (s, 0, 0))] * 2,
        out_specs=pl.BlockSpec((1, 8, 1, 2, BLOCK, WIDTH), lambda s: (s // 2, 0, s % 2, 0, 0, 0)),
        out_shape=jax.ShapeDtypeStruct((2, 8, 2, 2, BLOCK, WIDTH), bf16),
        cost_estimate=estimate(0, 4 << 20),
        name="pack_keys",
    )(keys, values)
    packed_q = [
        pl.pallas_call(
            pack_queries,
            grid=(2,),
            in_specs=[pl.BlockSpec((1, BLOCK, QUERY_HEADS * WIDTH), lambda p, turn=turn: (2 * p + turn, 0, 0))],
            out_specs=pl.BlockSpec((1, 16, 2, BLOCK, WIDTH), lambda p: (p, 0, 0, 0, 0)),
            out_shape=jax.ShapeDtypeStruct((2, 16, 2, BLOCK, WIDTH), bf16),
            cost_estimate=estimate(0, 4 << 20),
            name="pack_queries",
        )(queries)
        for turn in range(2)
    ]

    swap = [(i, i ^ 1) for i in range(RANKS)]
    onward = [(i, (i + 1) % 4) for i in range(4)]
    mine = lax.all_to_all(packed_kv.reshape(RANKS, 2 * BLOCK, WIDTH), "cp", 0, 0, tiled=True)
    mine_before = lax.ppermute(mine, "grp", onward)
    other = lax.ppermute(mine, "cp", swap)
    other_before = lax.ppermute(mine_before, "cp", swap)
    got_q = [
        lax.all_to_all(packed.reshape(RANKS, 2 * BLOCK, WIDTH), "cp", 0, 0, tiled=True) for packed in packed_q
    ]
    back = []
    for turn in range(2):
        info = jnp.stack([rank % 2, plane, rank // 16, turn]).astype(jnp.int32)
        result = attention(
            info, doc_lengths, got_q[turn].reshape(RANKS, 2, BLOCK, WIDTH), mine, other, mine_before, other_before
        )
        sent = lax.all_to_all(result.reshape(RANKS, 2 * BLOCK, WIDTH), "cp", 0, 0, tiled=True)
        back.append(sent.reshape(2, 16, 2, BLOCK, WIDTH))
    return pl.pallas_call(
        unpack_outputs,
        grid=(2,),
        in_specs=[pl.BlockSpec((1, 16, 2, BLOCK, WIDTH), lambda p: (p, 0, 0, 0, 0))] * 2,
        out_specs=pl.BlockSpec((2, BLOCK, QUERY_HEADS * WIDTH), lambda p: (p, 0, 0)),
        out_shape=jax.ShapeDtypeStruct((4, BLOCK, QUERY_HEADS * WIDTH), bf16),
        cost_estimate=estimate(0, 8 << 20),
        name="unpack_outputs",
    )(*back)


def solution(mesh):
    placed = P(None, ("grp", "cp"), None)
    return jax.shard_map(
        on_device,
        mesh=mesh,
        in_specs=(placed, placed, placed, P()),
        out_specs=placed,
        check_vma=False,
    )
```

```python
import jax
import jax.numpy as jnp
from jax import lax
from jax.experimental import pallas as pl
from jax.experimental.pallas import tpu as pltpu
from jax.sharding import PartitionSpec as P

QUERY_HEADS = 32
KEY_VALUE_HEADS = 8
WIDTH = 128
DOCS = 16
BLOCK = 128
RANKS = 32
CHUNK = RANKS * BLOCK
PAD = 512
TILE = 256
TILES = CHUNK // TILE
EDGE = 512
COLUMNS = EDGE // WIDTH
FACTOR = WIDTH ** (-0.5) * 1.4426950408889634
NEGATIVE = -1e30
LEAST = -(2**31)
LOW, HIGH = 1e-30, 1e30


def pack_keys(k_ref, v_ref, out_ref):
    for head in range(KEY_VALUE_HEADS):
        columns = slice(head * WIDTH, (head + 1) * WIDTH)
        out_ref[0, head, 0, 0] = k_ref[0, :, columns].T
        out_ref[0, head, 0, 1] = v_ref[0, :, columns]


def pack_queries(q_ref, even_ref, odd_ref):
    for turn, out_ref in enumerate((even_ref, odd_ref)):
        for head in range(QUERY_HEADS):
            out_ref[0, head // 2, head % 2] = q_ref[turn, :, head * WIDTH : (head + 1) * WIDTH]


def unpack_outputs(even_ref, odd_ref, out_ref):
    for turn, in_ref in enumerate((even_ref, odd_ref)):
        for head in range(QUERY_HEADS):
            out_ref[turn, :, head * WIDTH : (head + 1) * WIDTH] = in_ref[0, head // 2, head % 2]


def attend(info, lengths, q_ref, mine, other, mine_before, other_before, o_ref, kbuf, vbuf, probs, acc, sums, portion, lows, reach, top, ends, low_of, whole_of, docs_of, span_of, arrived):
    core, plane, pair, turn = info[0], info[1], info[2], info[3]
    stream = pair * 2 + turn
    base = (plane - 1) * CHUNK

    def fetch(before, now):
        copies = [
            pltpu.make_async_copy(source.at[:, pl.ds(half * BLOCK, BLOCK)], target.at[pl.ds(first, RANKS)], arrived.at[number])
            for number, (source, half, target, first) in enumerate(
                (
                    (before, 0, kbuf, PAD // BLOCK),
                    (now, 0, kbuf, PAD // BLOCK + RANKS),
                    (before, 1, vbuf, PAD // BLOCK),
                    (now, 1, vbuf, PAD // BLOCK + RANKS),
                )
            )
        ]
        for copy in copies:
            copy.start()
        for copy in copies:
            copy.wait()

    @pl.when(turn == core)
    def _():
        fetch(mine_before, mine)

    @pl.when(turn != core)
    def _():
        fetch(other_before, other)

    rows = lax.broadcasted_iota(jnp.int32, (2, BLOCK, WIDTH), 0) * BLOCK + lax.broadcasted_iota(
        jnp.int32, (2, BLOCK, WIDTH), 1
    )
    lanes = lax.broadcasted_iota(jnp.int32, (2, BLOCK, WIDTH), 2)

    kbuf[: PAD // BLOCK] = jnp.zeros((PAD // BLOCK, WIDTH, BLOCK), jnp.bfloat16)
    vbuf[: PAD // BLOCK] = jnp.zeros((PAD // BLOCK, BLOCK, WIDTH), jnp.bfloat16)
    acc[...] = jnp.zeros_like(acc)
    sums[...] = jnp.zeros_like(sums)
    probs[...] = jnp.zeros_like(probs)

    total = -base
    for doc in range(DOCS):
        total = total + lengths[stream, doc]
        ends[doc] = total

    def top_of(tile):
        return CHUNK + (tile + 1) * TILE - EDGE

    def survey(tile, blocks):
        begin = CHUNK + tile * TILE
        first, last, passed, within = -base, -base, 0, 0
        for doc in range(DOCS):
            end = ends[doc]
            first = jnp.where(end <= begin, end, first)
            last = jnp.where(end < begin + TILE, end, last)
            passed += (end <= begin).astype(jnp.int32)
            within += (end < begin + TILE).astype(jnp.int32)
        low = (first // TILE) * TILE
        low_of[tile] = low
        whole_of[tile] = last
        docs_of[0, tile] = first
        docs_of[1, tile] = passed
        docs_of[2, tile] = within
        return blocks + (begin + TILE - low + EDGE - 1) // EDGE

    blocks = lax.fori_loop(0, TILES, survey, 0)

    def prepare(tile):
        begin = CHUNK + tile * TILE
        first = docs_of[0, tile]
        lows[...] = (first + LEAST) - lanes
        reach[...] = rows + (begin - first + LEAST)

        def mark(doc, carry):
            end = ends[doc]
            inside = rows + begin >= end
            lows[...] = jnp.where(inside, (end + LEAST) - lanes, lows[...])
            reach[...] = jnp.where(inside, rows + (begin - end + LEAST), reach[...])
            return carry

        lax.fori_loop(docs_of[1, tile], docs_of[2, tile], mark, 0)

    def scores_of(tile, offset):
        at = (offset + PAD) // BLOCK
        queries = q_ref[pl.ds(tile * 2, 2)].reshape(4 * BLOCK, WIDTH)
        return [
            jnp.dot(
                queries,
                jnp.concatenate([kbuf[at + column], kbuf[at + column + 1]], axis=1),
                preferred_element_type=jnp.float32,
            )
            for column in range(0, COLUMNS, 2)
        ]

    def weigh(found, offset, uses_mask):
        for block in range(2):
            for row in range(0, BLOCK, 16):
                if uses_mask:
                    allowed = [
                        (offset + column * WIDTH) - lows[block, row : row + 16] <= reach[block, row : row + 16]
                        for column in range(COLUMNS)
                    ]
                for head in range(2):
                    rows_at = (block * 2 + head) * BLOCK + row
                    parts = []
                    for column in range(COLUMNS):
                        lane = column % 2 * WIDTH
                        part = found[column // 2][rows_at : rows_at + 16, lane : lane + WIDTH] * FACTOR
                        if uses_mask:
                            part = jnp.where(allowed[column], part, NEGATIVE)
                        part = jnp.exp2(part)
                        probs[column, rows_at : rows_at + 16] = part.astype(jnp.bfloat16)
                        parts.append(part)
                    sums[rows_at : rows_at + 16] += (parts[0] + parts[1]) + (parts[2] + parts[3])

    def product_of(offset):
        values = vbuf[pl.ds((offset + PAD) // BLOCK, EDGE // BLOCK)].reshape(EDGE, WIDTH)
        return [
            jnp.dot(
                jnp.concatenate([probs[column, half : half + 2 * BLOCK] for column in range(COLUMNS)], axis=1),
                values,
                preferred_element_type=jnp.float32,
            )
            for half in (0, 2 * BLOCK)
        ]

    def add(products):
        for half in range(2):
            acc[half * 2 * BLOCK : (half + 1) * 2 * BLOCK] += products[half]

    def close():
        total = jnp.sum(sums[...], axis=-1, keepdims=True)
        span_of[0] = jnp.minimum(span_of[0], jnp.min(total.reshape(64, 8, 1), axis=0))
        span_of[1] = jnp.maximum(span_of[1], jnp.max(total.reshape(64, 8, 1), axis=0))
        portion[...] = jnp.broadcast_to(1.0 / total, (4 * BLOCK, WIDTH))
        sums[...] = jnp.zeros_like(sums)

    def finish(tile):
        o_ref[pl.ds(tile * 2, 2)] = (acc[...] * portion[...]).astype(jnp.bfloat16).reshape(2, 2, BLOCK, WIDTH)
        acc[...] = jnp.zeros_like(acc)

    def fast(step, carry):
        tile, offset, tile_before, offset_before, closes = carry

        def both(uses_mask):
            found = scores_of(tile, offset)
            products = product_of(offset_before)
            weigh(found, offset, uses_mask)
            add(products)

        plain = (offset >= whole_of[tile]) & (offset < top_of(tile))

        @pl.when(plain)
        def _():
            both(False)

        @pl.when(jnp.logical_not(plain))
        def _():
            both(True)

        @pl.when(closes == 1)
        def _():
            finish(tile_before)

        ended = (offset <= low_of[tile]).astype(jnp.int32)
        tile_next = jnp.minimum(tile + ended, TILES - 1)
        offset_next = jnp.where(ended == 1, top_of(tile_next), offset - EDGE)

        @pl.when(ended == 1)
        def _():
            close()
            prepare(tile_next)

        return tile_next, offset_next, tile, offset, ended

    def slow(tile, carry):
        begin = CHUNK + tile * TILE
        prepare(tile)
        acc[...] = jnp.zeros_like(acc)
        sums[...] = jnp.zeros_like(sums)
        top[...] = jnp.full_like(top, NEGATIVE)

        def absorb(step, carry):
            offset = top_of(tile) - step * EDGE
            found = scores_of(tile, offset)
            for piece in range(4):
                at = slice(piece * BLOCK, (piece + 1) * BLOCK)
                parts = []
                for column in range(COLUMNS):
                    lane = column % 2 * WIDTH
                    part = found[column // 2][at, lane : lane + WIDTH]
                    allowed = (offset + column * WIDTH) - lows[piece // 2] <= reach[piece // 2]
                    parts.append(jnp.where(allowed, part * FACTOR, NEGATIVE))
                before = top[at]
                highest = jnp.maximum(jnp.maximum(parts[0], parts[1]), jnp.maximum(parts[2], parts[3]))
                peak = jnp.maximum(before, jnp.max(highest, axis=-1, keepdims=True))
                shrink = jnp.exp2(before - peak)
                total = jnp.zeros((BLOCK, WIDTH), jnp.float32)
                for column in range(COLUMNS):
                    part = jnp.where(parts[column] > 0.5 * NEGATIVE, jnp.exp2(parts[column] - peak), 0.0)
                    probs[column, at] = part.astype(jnp.bfloat16)
                    total = total + part
                sums[at] = sums[at] * shrink + total
                acc[at] = acc[at] * shrink
                top[at] = peak
            add(product_of(offset))
            return carry

        lax.fori_loop(0, (begin + TILE - low_of[tile] + EDGE - 1) // EDGE, absorb, 0)
        close()
        finish(tile)
        return carry

    span_of[0] = jnp.full((8, WIDTH), 1.0, jnp.float32)
    span_of[1] = jnp.full((8, WIDTH), 1.0, jnp.float32)
    prepare(0)
    lax.fori_loop(0, blocks + 1, fast, (0, top_of(0), 0, top_of(0), 0))
    fits = (jnp.min(span_of[0]) >= LOW) & (jnp.max(span_of[1]) <= HIGH)

    @pl.when(jnp.logical_not(fits))
    def _():
        lax.fori_loop(0, TILES, slow, 0)


def estimate(flops, moved, powers=0):
    return pl.CostEstimate(flops=flops, bytes_accessed=moved, transcendentals=powers)


def attention(info, doc_lengths, *arrays):
    anywhere = pl.BlockSpec(memory_space=pl.ANY)
    half = pl.BlockSpec((RANKS, 2, BLOCK, WIDTH), lambda u, *_: (0, 0, 0, 0), pipeline_mode=pl.Buffered(1))
    return pl.pallas_call(
        attend,
        grid_spec=pltpu.PrefetchScalarGridSpec(
            num_scalar_prefetch=2,
            grid=(1,),
            in_specs=[half, anywhere, anywhere, anywhere, anywhere],
            out_specs=half,
            scratch_shapes=[
                pltpu.VMEM(((PAD + 2 * CHUNK) // BLOCK, WIDTH, BLOCK), jnp.bfloat16),
                pltpu.VMEM(((PAD + 2 * CHUNK) // BLOCK, BLOCK, WIDTH), jnp.bfloat16),
                pltpu.VMEM((COLUMNS, 4 * BLOCK, WIDTH), jnp.bfloat16),
                pltpu.VMEM((4 * BLOCK, WIDTH), jnp.float32),
                pltpu.VMEM((4 * BLOCK, WIDTH), jnp.float32),
                pltpu.VMEM((4 * BLOCK, WIDTH), jnp.float32),
                pltpu.VMEM((2, BLOCK, WIDTH), jnp.int32),
                pltpu.VMEM((2, BLOCK, WIDTH), jnp.int32),
                pltpu.VMEM((4 * BLOCK, WIDTH), jnp.float32),
                pltpu.SMEM((DOCS,), jnp.int32),
                pltpu.SMEM((TILES,), jnp.int32),
                pltpu.SMEM((TILES,), jnp.int32),
                pltpu.SMEM((3, TILES), jnp.int32),
                pltpu.VMEM((2, 8, WIDTH), jnp.float32),
                pltpu.SemaphoreType.DMA((4,)),
            ],
        ),
        out_shape=jax.ShapeDtypeStruct((RANKS, 2, BLOCK, WIDTH), jnp.bfloat16),
        cost_estimate=estimate(20 << 30, 8 << 20, 10 << 20),
        compiler_params=pltpu.CompilerParams(vmem_limit_bytes=60 << 20),
        name="attend",
    )(info, doc_lengths, *arrays)


def on_device(queries, keys, values, doc_lengths):
    rank = lax.axis_index("cp")
    plane = lax.axis_index("grp")
    bf16 = jnp.bfloat16

    packed_kv = pl.pallas_call(
        pack_keys,
        grid=(4,),
        in_specs=[pl.BlockSpec((1, BLOCK, KEY_VALUE_HEADS * WIDTH), lambda s: (s, 0, 0))] * 2,
        out_specs=pl.BlockSpec((1, 8, 1, 2, BLOCK, WIDTH), lambda s: (s // 2, 0, s % 2, 0, 0, 0)),
        out_shape=jax.ShapeDtypeStruct((2, 8, 2, 2, BLOCK, WIDTH), bf16),
        cost_estimate=estimate(0, 4 << 20),
        name="pack_keys",
    )(keys, values)
    packed_q = pl.pallas_call(
        pack_queries,
        grid=(2,),
        in_specs=[pl.BlockSpec((2, BLOCK, QUERY_HEADS * WIDTH), lambda p: (p, 0, 0))],
        out_specs=[pl.BlockSpec((1, 16, 2, BLOCK, WIDTH), lambda p: (p, 0, 0, 0, 0))] * 2,
        out_shape=[jax.ShapeDtypeStruct((2, 16, 2, BLOCK, WIDTH), bf16)] * 2,
        cost_estimate=estimate(0, 8 << 20),
        name="pack_queries",
    )(queries)

    swap = [(i, i ^ 1) for i in range(RANKS)]
    onward = [(i, (i + 1) % 4) for i in range(4)]
    mine = lax.all_to_all(packed_kv.reshape(RANKS, 2 * BLOCK, WIDTH), "cp", 0, 0, tiled=True)
    mine_before = lax.ppermute(mine, "grp", onward)
    other = lax.ppermute(mine, "cp", swap)
    got_q = []
    for packed in packed_q:
        got_q.append(lax.all_to_all(packed.reshape(RANKS, 2 * BLOCK, WIDTH), "cp", 0, 0, tiled=True))
    other_before = lax.ppermute(mine_before, "cp", swap)
    back = []
    for turn in range(2):
        info = jnp.stack([rank % 2, plane, rank // 16, turn]).astype(jnp.int32)
        result = attention(
            info, doc_lengths, got_q[turn].reshape(RANKS, 2, BLOCK, WIDTH), mine, other, mine_before, other_before
        )
        sent = lax.all_to_all(result.reshape(RANKS, 2 * BLOCK, WIDTH), "cp", 0, 0, tiled=True)
        back.append(sent.reshape(2, 16, 2, BLOCK, WIDTH))
    return pl.pallas_call(
        unpack_outputs,
        grid=(2,),
        in_specs=[pl.BlockSpec((1, 16, 2, BLOCK, WIDTH), lambda p: (p, 0, 0, 0, 0))] * 2,
        out_specs=pl.BlockSpec((2, BLOCK, QUERY_HEADS * WIDTH), lambda p: (p, 0, 0)),
        out_shape=jax.ShapeDtypeStruct((4, BLOCK, QUERY_HEADS * WIDTH), bf16),
        cost_estimate=estimate(0, 8 << 20),
        name="unpack_outputs",
    )(*back)


def solution(mesh):
    placed = P(None, ("grp", "cp"), None)
    return jax.shard_map(
        on_device,
        mesh=mesh,
        in_specs=(placed, placed, placed, P()),
        out_specs=placed,
        check_vma=False,
    )
```

```python
import jax
import jax.numpy as jnp
from jax import lax
from jax.experimental import pallas as pl
from jax.experimental.pallas import tpu as pltpu
from jax.sharding import PartitionSpec as P

QUERY_HEADS = 32
KEY_VALUE_HEADS = 8
WIDTH = 128
DOCS = 16
BLOCK = 128
RANKS = 32
CHUNK = RANKS * BLOCK
PAD = 512
TILE = 256
TILES = CHUNK // TILE
EDGE = 512
COLUMNS = EDGE // WIDTH
FACTOR = WIDTH ** (-0.5) * 1.4426950408889634
NEGATIVE = -1e30
LEAST = -(2**31)
LOW, HIGH = 1e-30, 1e30


def pack_keys(k_ref, v_ref, out_ref):
    for head in range(KEY_VALUE_HEADS):
        columns = slice(head * WIDTH, (head + 1) * WIDTH)
        out_ref[0, head, 0, 0] = k_ref[0, :, columns].T
        out_ref[0, head, 0, 1] = v_ref[0, :, columns]


def swapped(info, lengths, pair):
    plane = info[1]

    def work(stream):
        total, begin = 0, 0
        for doc in range(DOCS):
            length = lengths[stream, doc]
            low = jnp.maximum(plane * CHUNK - begin, 0)
            high = jnp.minimum((plane + 1) * CHUNK - begin, length)
            total += jnp.where(high > low, high * high - low * low, 0)
            begin += length
        return total

    return (work(2 * pair + 1) > work(2 * pair)).astype(jnp.int32)


def pack_queries(info, lengths, q_ref, first_ref, second_ref):
    swap = swapped(info, lengths, pl.program_id(0))
    for turn, out_ref in enumerate((first_ref, second_ref)):
        stream = jnp.where(swap == 1, 1 - turn, turn)
        for head in range(QUERY_HEADS):
            out_ref[0, head // 2, head % 2] = q_ref[stream, :, head * WIDTH : (head + 1) * WIDTH]


def unpack_outputs(info, lengths, first_ref, second_ref, out_ref):
    swap = swapped(info, lengths, pl.program_id(0))
    for turn, in_ref in enumerate((first_ref, second_ref)):
        stream = jnp.where(swap == 1, 1 - turn, turn)
        for head in range(QUERY_HEADS):
            out_ref[stream, :, head * WIDTH : (head + 1) * WIDTH] = in_ref[0, head // 2, head % 2]


def attend(info, lengths, q_ref, mine, other, mine_before, other_before, o_ref, kbuf, vbuf, probs, acc, sums, portion, lows, reach, top, ends, low_of, whole_of, docs_of, span_of, arrived):
    core, plane, pair = info[0], info[1], info[2]
    swap = swapped(info, lengths, pair)
    turn = jnp.where(swap == 1, 1 - info[3], info[3])
    stream = pair * 2 + turn
    base = (plane - 1) * CHUNK

    def fetch(before, now):
        copies = [
            pltpu.make_async_copy(source.at[:, pl.ds(half * BLOCK, BLOCK)], target.at[pl.ds(first, RANKS)], arrived.at[number])
            for number, (source, half, target, first) in enumerate(
                (
                    (before, 0, kbuf, PAD // BLOCK),
                    (now, 0, kbuf, PAD // BLOCK + RANKS),
                    (before, 1, vbuf, PAD // BLOCK),
                    (now, 1, vbuf, PAD // BLOCK + RANKS),
                )
            )
        ]
        for copy in copies:
            copy.start()
        for copy in copies:
            copy.wait()

    @pl.when(turn == core)
    def _():
        fetch(mine_before, mine)

    @pl.when(turn != core)
    def _():
        fetch(other_before, other)

    rows = lax.broadcasted_iota(jnp.int32, (2, BLOCK, WIDTH), 0) * BLOCK + lax.broadcasted_iota(
        jnp.int32, (2, BLOCK, WIDTH), 1
    )
    lanes = lax.broadcasted_iota(jnp.int32, (2, BLOCK, WIDTH), 2)

    kbuf[: PAD // BLOCK] = jnp.zeros((PAD // BLOCK, WIDTH, BLOCK), jnp.bfloat16)
    vbuf[: PAD // BLOCK] = jnp.zeros((PAD // BLOCK, BLOCK, WIDTH), jnp.bfloat16)
    acc[...] = jnp.zeros_like(acc)
    sums[...] = jnp.zeros_like(sums)
    probs[...] = jnp.zeros_like(probs)

    total = -base
    for doc in range(DOCS):
        total = total + lengths[stream, doc]
        ends[doc] = total

    def top_of(tile):
        return CHUNK + (tile + 1) * TILE - EDGE

    def survey(tile, blocks):
        begin = CHUNK + tile * TILE
        first, last, passed, within = -base, -base, 0, 0
        for doc in range(DOCS):
            end = ends[doc]
            first = jnp.where(end <= begin, end, first)
            last = jnp.where(end < begin + TILE, end, last)
            passed += (end <= begin).astype(jnp.int32)
            within += (end < begin + TILE).astype(jnp.int32)
        low = (first // TILE) * TILE
        low_of[tile] = low
        whole_of[tile] = last
        docs_of[0, tile] = first
        docs_of[1, tile] = passed
        docs_of[2, tile] = within
        return blocks + (begin + TILE - low + EDGE - 1) // EDGE

    blocks = lax.fori_loop(0, TILES, survey, 0)

    def prepare(tile):
        begin = CHUNK + tile * TILE
        first = docs_of[0, tile]
        lows[...] = (first + LEAST) - lanes
        reach[...] = rows + (begin - first + LEAST)

        def mark(doc, carry):
            end = ends[doc]
            inside = rows + begin >= end
            lows[...] = jnp.where(inside, (end + LEAST) - lanes, lows[...])
            reach[...] = jnp.where(inside, rows + (begin - end + LEAST), reach[...])
            return carry

        lax.fori_loop(docs_of[1, tile], docs_of[2, tile], mark, 0)

    def scores_of(tile, offset):
        at = (offset + PAD) // BLOCK
        queries = q_ref[pl.ds(tile * 2, 2)].reshape(4 * BLOCK, WIDTH)
        return [
            jnp.dot(
                queries,
                jnp.concatenate([kbuf[at + column], kbuf[at + column + 1]], axis=1),
                preferred_element_type=jnp.float32,
            )
            for column in range(0, COLUMNS, 2)
        ]

    def weigh(found, offset, uses_mask):
        for block in range(2):
            for row in range(0, BLOCK, 16):
                if uses_mask:
                    allowed = [
                        (offset + column * WIDTH) - lows[block, row : row + 16] <= reach[block, row : row + 16]
                        for column in range(COLUMNS)
                    ]
                for head in range(2):
                    rows_at = (block * 2 + head) * BLOCK + row
                    parts = []
                    for column in range(COLUMNS):
                        lane = column % 2 * WIDTH
                        part = found[column // 2][rows_at : rows_at + 16, lane : lane + WIDTH] * FACTOR
                        if uses_mask:
                            part = jnp.where(allowed[column], part, NEGATIVE)
                        part = jnp.exp2(part)
                        probs[column, rows_at : rows_at + 16] = part.astype(jnp.bfloat16)
                        parts.append(part)
                    sums[rows_at : rows_at + 16] += (parts[0] + parts[1]) + (parts[2] + parts[3])

    def product_of(offset):
        values = vbuf[pl.ds((offset + PAD) // BLOCK, EDGE // BLOCK)].reshape(EDGE, WIDTH)
        return [
            jnp.dot(
                jnp.concatenate([probs[column, half : half + 2 * BLOCK] for column in range(COLUMNS)], axis=1),
                values,
                preferred_element_type=jnp.float32,
            )
            for half in (0, 2 * BLOCK)
        ]

    def add(products):
        for half in range(2):
            acc[half * 2 * BLOCK : (half + 1) * 2 * BLOCK] += products[half]

    def close():
        total = jnp.sum(sums[...], axis=-1, keepdims=True)
        span_of[0] = jnp.minimum(span_of[0], jnp.min(total.reshape(64, 8, 1), axis=0))
        span_of[1] = jnp.maximum(span_of[1], jnp.max(total.reshape(64, 8, 1), axis=0))
        portion[...] = jnp.broadcast_to(1.0 / total, (4 * BLOCK, WIDTH))
        sums[...] = jnp.zeros_like(sums)

    def finish(tile):
        o_ref[pl.ds(tile * 2, 2)] = (acc[...] * portion[...]).astype(jnp.bfloat16).reshape(2, 2, BLOCK, WIDTH)
        acc[...] = jnp.zeros_like(acc)

    def fast(step, carry):
        tile, offset, tile_before, offset_before, closes = carry

        def both(uses_mask):
            found = scores_of(tile, offset)
            products = product_of(offset_before)
            weigh(found, offset, uses_mask)
            add(products)

        plain = (offset >= whole_of[tile]) & (offset < top_of(tile))

        @pl.when(plain)
        def _():
            both(False)

        @pl.when(jnp.logical_not(plain))
        def _():
            both(True)

        @pl.when(closes == 1)
        def _():
            finish(tile_before)

        ended = (offset <= low_of[tile]).astype(jnp.int32)
        tile_next = jnp.minimum(tile + ended, TILES - 1)
        offset_next = jnp.where(ended == 1, top_of(tile_next), offset - EDGE)

        @pl.when(ended == 1)
        def _():
            close()
            prepare(tile_next)

        return tile_next, offset_next, tile, offset, ended

    def slow(tile, carry):
        begin = CHUNK + tile * TILE
        prepare(tile)
        acc[...] = jnp.zeros_like(acc)
        sums[...] = jnp.zeros_like(sums)
        top[...] = jnp.full_like(top, NEGATIVE)

        def absorb(step, carry):
            offset = top_of(tile) - step * EDGE
            found = scores_of(tile, offset)
            for piece in range(4):
                at = slice(piece * BLOCK, (piece + 1) * BLOCK)
                parts = []
                for column in range(COLUMNS):
                    lane = column % 2 * WIDTH
                    part = found[column // 2][at, lane : lane + WIDTH]
                    allowed = (offset + column * WIDTH) - lows[piece // 2] <= reach[piece // 2]
                    parts.append(jnp.where(allowed, part * FACTOR, NEGATIVE))
                before = top[at]
                highest = jnp.maximum(jnp.maximum(parts[0], parts[1]), jnp.maximum(parts[2], parts[3]))
                peak = jnp.maximum(before, jnp.max(highest, axis=-1, keepdims=True))
                shrink = jnp.exp2(before - peak)
                total = jnp.zeros((BLOCK, WIDTH), jnp.float32)
                for column in range(COLUMNS):
                    part = jnp.where(parts[column] > 0.5 * NEGATIVE, jnp.exp2(parts[column] - peak), 0.0)
                    probs[column, at] = part.astype(jnp.bfloat16)
                    total = total + part
                sums[at] = sums[at] * shrink + total
                acc[at] = acc[at] * shrink
                top[at] = peak
            add(product_of(offset))
            return carry

        lax.fori_loop(0, (begin + TILE - low_of[tile] + EDGE - 1) // EDGE, absorb, 0)
        close()
        finish(tile)
        return carry

    span_of[0] = jnp.full((8, WIDTH), 1.0, jnp.float32)
    span_of[1] = jnp.full((8, WIDTH), 1.0, jnp.float32)
    prepare(0)
    lax.fori_loop(0, blocks + 1, fast, (0, top_of(0), 0, top_of(0), 0))
    fits = (jnp.min(span_of[0]) >= LOW) & (jnp.max(span_of[1]) <= HIGH)

    @pl.when(jnp.logical_not(fits))
    def _():
        lax.fori_loop(0, TILES, slow, 0)


def estimate(flops, moved, powers=0):
    return pl.CostEstimate(flops=flops, bytes_accessed=moved, transcendentals=powers)


def attention(info, doc_lengths, *arrays):
    anywhere = pl.BlockSpec(memory_space=pl.ANY)
    half = pl.BlockSpec((RANKS, 2, BLOCK, WIDTH), lambda u, *_: (0, 0, 0, 0), pipeline_mode=pl.Buffered(1))
    return pl.pallas_call(
        attend,
        grid_spec=pltpu.PrefetchScalarGridSpec(
            num_scalar_prefetch=2,
            grid=(1,),
            in_specs=[half, anywhere, anywhere, anywhere, anywhere],
            out_specs=half,
            scratch_shapes=[
                pltpu.VMEM(((PAD + 2 * CHUNK) // BLOCK, WIDTH, BLOCK), jnp.bfloat16),
                pltpu.VMEM(((PAD + 2 * CHUNK) // BLOCK, BLOCK, WIDTH), jnp.bfloat16),
                pltpu.VMEM((COLUMNS, 4 * BLOCK, WIDTH), jnp.bfloat16),
                pltpu.VMEM((4 * BLOCK, WIDTH), jnp.float32),
                pltpu.VMEM((4 * BLOCK, WIDTH), jnp.float32),
                pltpu.VMEM((4 * BLOCK, WIDTH), jnp.float32),
                pltpu.VMEM((2, BLOCK, WIDTH), jnp.int32),
                pltpu.VMEM((2, BLOCK, WIDTH), jnp.int32),
                pltpu.VMEM((4 * BLOCK, WIDTH), jnp.float32),
                pltpu.SMEM((DOCS,), jnp.int32),
                pltpu.SMEM((TILES,), jnp.int32),
                pltpu.SMEM((TILES,), jnp.int32),
                pltpu.SMEM((3, TILES), jnp.int32),
                pltpu.VMEM((2, 8, WIDTH), jnp.float32),
                pltpu.SemaphoreType.DMA((4,)),
            ],
        ),
        out_shape=jax.ShapeDtypeStruct((RANKS, 2, BLOCK, WIDTH), jnp.bfloat16),
        cost_estimate=estimate(20 << 30, 8 << 20, 10 << 20),
        compiler_params=pltpu.CompilerParams(vmem_limit_bytes=60 << 20),
        name="attend",
    )(info, doc_lengths, *arrays)


def on_device(queries, keys, values, doc_lengths):
    rank = lax.axis_index("cp")
    plane = lax.axis_index("grp")
    bf16 = jnp.bfloat16

    packed_kv = pl.pallas_call(
        pack_keys,
        grid=(4,),
        in_specs=[pl.BlockSpec((1, BLOCK, KEY_VALUE_HEADS * WIDTH), lambda s: (s, 0, 0))] * 2,
        out_specs=pl.BlockSpec((1, 8, 1, 2, BLOCK, WIDTH), lambda s: (s // 2, 0, s % 2, 0, 0, 0)),
        out_shape=jax.ShapeDtypeStruct((2, 8, 2, 2, BLOCK, WIDTH), bf16),
        cost_estimate=estimate(0, 4 << 20),
        name="pack_keys",
    )(keys, values)
    infos = [jnp.stack([rank % 2, plane, rank // 16, jnp.int32(turn)]).astype(jnp.int32) for turn in range(2)]
    packed_q = pl.pallas_call(
        pack_queries,
        grid_spec=pltpu.PrefetchScalarGridSpec(
            num_scalar_prefetch=2,
            grid=(2,),
            in_specs=[pl.BlockSpec((2, BLOCK, QUERY_HEADS * WIDTH), lambda p, *_: (p, 0, 0))],
            out_specs=[pl.BlockSpec((1, 16, 2, BLOCK, WIDTH), lambda p, *_: (p, 0, 0, 0, 0))] * 2,
        ),
        out_shape=[jax.ShapeDtypeStruct((2, 16, 2, BLOCK, WIDTH), bf16)] * 2,
        cost_estimate=estimate(0, 8 << 20),
        name="pack_queries",
    )(infos[0], doc_lengths, queries)

    swap = [(i, i ^ 1) for i in range(RANKS)]
    onward = [(i, (i + 1) % 4) for i in range(4)]
    mine = lax.all_to_all(packed_kv.reshape(RANKS, 2 * BLOCK, WIDTH), "cp", 0, 0, tiled=True)
    mine_before = lax.ppermute(mine, "grp", onward)
    other = lax.ppermute(mine, "cp", swap)
    got_q = []
    for packed in packed_q:
        got_q.append(lax.all_to_all(packed.reshape(RANKS, 2 * BLOCK, WIDTH), "cp", 0, 0, tiled=True))
    other_before = lax.ppermute(mine_before, "cp", swap)
    back = []
    for turn in range(2):
        result = attention(
            infos[turn], doc_lengths, got_q[turn].reshape(RANKS, 2, BLOCK, WIDTH), mine, other, mine_before, other_before
        )
        sent = lax.all_to_all(result.reshape(RANKS, 2 * BLOCK, WIDTH), "cp", 0, 0, tiled=True)
        back.append(sent.reshape(2, 16, 2, BLOCK, WIDTH))
    return pl.pallas_call(
        unpack_outputs,
        grid_spec=pltpu.PrefetchScalarGridSpec(
            num_scalar_prefetch=2,
            grid=(2,),
            in_specs=[pl.BlockSpec((1, 16, 2, BLOCK, WIDTH), lambda p, *_: (p, 0, 0, 0, 0))] * 2,
            out_specs=pl.BlockSpec((2, BLOCK, QUERY_HEADS * WIDTH), lambda p, *_: (p, 0, 0)),
        ),
        out_shape=jax.ShapeDtypeStruct((4, BLOCK, QUERY_HEADS * WIDTH), bf16),
        cost_estimate=estimate(0, 8 << 20),
        name="unpack_outputs",
    )(infos[0], doc_lengths, *back)


def solution(mesh):
    placed = P(None, ("grp", "cp"), None)
    return jax.shard_map(
        on_device,
        mesh=mesh,
        in_specs=(placed, placed, placed, P()),
        out_specs=placed,
        check_vma=False,
    )
```
